256 devices in a mesh: layer: 32 (over y, z), row: 2 (over core), col: 4 (over x).
Axes of the slice: x: 4, y: 4, z: 8, core: 2. Of those that a mesh axis runs over, the one named last changes fastest.
Arguments:
- lpanel: bfloat16 [32, 8, 3072, 256], P('layer', None, 'row', 'col'), may hold values from -6 to 6
- upanel: bfloat16 [32, 8, 256, 3072], P('layer', None, 'row', 'col'), may hold values from -0.03125 to 0.03125
- lpat: int32 [32, 8, 24], P('layer', None, 'row'), may hold values 0 or 1
- upat: int32 [32, 8, 24], P('layer', None, 'col'), may hold values 0 or 1
- ancestor_entries: float32 [3072, 3072], P('row', 'col'), may hold values from -2 to 64, as said below
Outputs:
- schur: float32 [3072, 3072], P(('row', 'layer'), 'col')
- diag_lu: float32 [24, 128, 128], P('col')
The draws below stay inside these ranges and needn't reach their ends.
Inputs may be any that keep to these rules, and one draw needn't show every extreme that they name: `ancestor_entries`: entries on the diagonal lie in 32 to 64; all other entries in -2 to 2.
All inputs are finite; a program needn't handle non-finite values. No bound on the sum of `lpat` or of `upat` on one device may be relied on, other than what follows from the above.
Results may differ from the reference program's by a relative error of at most 0.0003.
Values may be sent and summed in bfloat16 or wider, within the bound.
A program may use at most 64 MiB of HBM per device.

```python
import jax
import jax.numpy as jnp
from jax import lax

A = 3072
W = 256
BLK = 128
SUPER = 8
LAYERS = 32
NB = 24


def draw_ancestor_entries(key, part):
    first = jax.random.fold_in(key, 11)
    second = jax.random.fold_in(key, 12)
    others = 0.3 * jnp.clip(jax.random.normal(first, (A, A), jnp.float32), -6.0, 6.0)
    diagonal = jax.random.uniform(second, (A,), jnp.float32, 32.0, 64.0)
    rows_index = jnp.arange(A)[:, None]
    cols_index = jnp.arange(A)[None, :]
    return jnp.where(rows_index == cols_index, diagonal[:, None], others).astype(jnp.float32)


def plant(entries, stream_key, least, top_value):
    extent = entries.shape
    spot = [jax.random.randint(jax.random.fold_in(stream_key, axis), (), 0, extent[axis]) for axis in range(len(extent))]
    entries = entries.at[tuple(spot)].set(least)
    longest = extent.index(max(extent))
    spot[longest] = (spot[longest] + 1) % extent[longest]
    return entries.at[tuple(spot)].set(top_value)


def spiked(values, own_key, source, target, shards_of, factor):
    def block_of(axis_at):
        return (jnp.arange(values.shape[axis_at]) // (values.shape[axis_at] // shards_of)).reshape((-1,) + (1,) * (values.ndim - 1 - axis_at))

    one_side = jax.random.permutation(own_key, shards_of)[block_of(target)]
    far = (block_of(target) + shards_of // 2) % shards_of
    return jnp.where((block_of(source) == one_side) | (block_of(source) == far), factor * values, values)


def shard_levels(rng, shape, pieces, low, high):
    level, own = 1.0, jax.random.fold_in(rng, 6)
    for axis_at, parts in pieces:
        draws = jnp.exp(jax.random.uniform(jax.random.fold_in(own, axis_at), (parts,), jnp.float32, low / len(pieces), high / len(pieces)))
        level = level * jnp.repeat(draws, shape[axis_at] // parts).reshape([-1 if axis == axis_at else 1 for axis in range(len(shape))])
    return level


def gaussian(own_key, extent, deviation, limit, cuts=(), dtype=jnp.bfloat16):
    entries = deviation * jax.random.normal(own_key, extent, jnp.float32)
    if cuts:
        entries = entries * shard_levels(own_key, extent, cuts, -0.22, 0.18)
    return jnp.clip(entries, -limit, limit).astype(dtype)


def gaussian_with(rng, dims, scale, limit, split, heavy, held_as=jnp.bfloat16):
    result = scale * jax.random.normal(rng, dims, jnp.float32)
    if split:
        result = result * shard_levels(rng, dims, split, -0.22, 0.18)
    return jnp.clip(spiked(result, jax.random.fold_in(rng, 3), *heavy), -limit, limit).astype(held_as)


def setup_inputs(seed: int = 0) -> dict:
    streams_of = jax.random.split(jax.random.key(seed), 6)
    lpanel = gaussian_with(streams_of[0], (LAYERS, SUPER, A, W), 1.0, 6.0, ((0, 32), (2, 2), (3, 4)), (0, 2, 32, 2.75))
    upanel = gaussian(streams_of[1], (LAYERS, SUPER, W, A), (0.6 / (LAYERS * SUPER * W) ** 0.5), 0.03125, ((0, 32), (2, 2), (3, 4)))
    lpat = plant((jax.random.randint(streams_of[2], (LAYERS, SUPER, NB), 0, 4) < 3).astype(jnp.int32), jax.random.fold_in(streams_of[2], 1), 0, 1)
    upat = plant((jax.random.randint(streams_of[3], (LAYERS, SUPER, NB), 0, 4) < 3).astype(jnp.int32), jax.random.fold_in(streams_of[3], 1), 0, 1)
    ancestor_entries = draw_ancestor_entries(jax.random.fold_in(streams_of[5], 71), 0)
    return {"lpanel": lpanel, "upanel": upanel, "lpat": lpat, "upat": upat, "ancestor_entries": ancestor_entries}


def eliminate(tile, steps):
    size = tile.shape[-1]
    places = jnp.arange(size)

    def sweep(step, current):
        pivot = current[:, step, step]
        below = places > step
        column = jnp.where(below[None, :], current[:, :, step] / pivot[:, None], 0.0)
        row_part = jnp.where(below[None, :], current[:, step, :], 0.0)
        current = current - column[:, :, None] * row_part[:, None, :]
        placed = below[None, :, None] & (places == step)[None, None, :]
        return jnp.where(placed, column[:, :, None], current)

    return lax.fori_loop(0, steps, sweep, tile)


def reference(lpanel, upanel, lpat, upat, ancestor_entries):
    def layer_term(total, items):
        left, right, left_pattern, right_pattern = items
        left = (left.reshape(SUPER, NB, BLK, W) * left_pattern[:, :, None, None].astype(jnp.bfloat16)).reshape(SUPER, A, W)
        right = (right.reshape(SUPER, W, NB, BLK) * right_pattern[:, None, :, None].astype(jnp.bfloat16)).reshape(SUPER, W, A)
        left_flat = jnp.transpose(left, (1, 0, 2)).reshape(A, SUPER * W).astype(jnp.float32)
        right_flat = right.reshape(SUPER * W, A).astype(jnp.float32)
        product = jnp.dot(left_flat, right_flat, precision=lax.Precision.HIGHEST, preferred_element_type=jnp.float32)
        return total + product, None

    total = lax.scan(layer_term, jnp.zeros((A, A), jnp.float32), (lpanel, upanel, lpat, upat))[0]
    schur = ancestor_entries - total
    shaped = schur.reshape(NB, BLK, NB, BLK)
    blocks = jnp.moveaxis(jnp.diagonal(shaped, axis1=0, axis2=2), -1, 0)
    return schur, eliminate(blocks, BLK)
```

```python
import jax
import jax.numpy as jnp
from jax import lax
from jax.experimental import pallas as pl
from jax.experimental.pallas import tpu as pltpu
from jax.sharding import PartitionSpec as P

BLK = 128
SEGMENTS = 4


def lu_blocks(ref, count):
    lanes = lax.broadcasted_iota(jnp.int32, (1, BLK), 1)
    span = BLK // SEGMENTS
    for segment in range(SEGMENTS):
        top = segment * span
        height = BLK - top
        rows = top + lax.broadcasted_iota(jnp.int32, (height, 1), 0)

        def panel(index, carry):
            first = top + index * 8
            for j in range(8):
                keep = jnp.logical_and(lanes > j, lanes + first < BLK)
                below = rows > first + j
                for b in range(count):
                    row = ref[b, pl.ds(first + j, 1), :]
                    inverse = 1.0 / row[:, j : j + 1]
                    current = ref[b, top:, :]
                    factors = jnp.where(below, current[:, j : j + 1] * inverse, 0.0)
                    updated = current - factors * jnp.where(keep, row, 0.0)
                    placed = jnp.logical_and(below, lanes == j)
                    ref[b, top:, :] = jnp.where(placed, factors, updated)
            for b in range(count):
                ref[b] = pltpu.roll(ref[b], BLK - 8, 1)
            return carry

        lax.fori_loop(0, span // 8, panel, 0)


def lu_kernel(blocks_ref, out_ref):
    out_ref[...] = blocks_ref[...]
    lu_blocks(out_ref, out_ref.shape[0])


def factor(blocks):
    return pl.pallas_call(
        lu_kernel,
        out_shape=jax.ShapeDtypeStruct(blocks.shape, jnp.float32),
        in_specs=[pl.BlockSpec(memory_space=pltpu.VMEM)],
        out_specs=pl.BlockSpec(memory_space=pltpu.VMEM),
    )(blocks)


def mask_rows(panel, pattern, block):
    count, length, inner = panel.shape
    shaped = panel.reshape(count, length // block, block, inner)
    return (shaped * pattern[:, :, None, None].astype(panel.dtype)).reshape(count, length, inner)


def mask_cols(panel, pattern, block):
    count, inner, length = panel.shape
    shaped = panel.reshape(count, inner, length // block, block)
    return (shaped * pattern[:, None, :, None].astype(panel.dtype)).reshape(count, inner, length)


def diagonal(matrix):
    width = matrix.shape[1]
    per_group = lax.axis_size("col") // lax.axis_size("row")
    column = lax.axis_index("col")
    valid = column // per_group == lax.axis_index("row")
    square = lax.dynamic_slice_in_dim(matrix, column % per_group * width, width, 0)
    blocks = jnp.stack(
        [square[j * BLK : (j + 1) * BLK, j * BLK : (j + 1) * BLK] for j in range(width // BLK)]
    )
    return jnp.where(valid, blocks, 0.0)


def shards(lpanel, upanel, lpat, upat, ancestor_entries):
    left_masked = mask_rows(lpanel[0], lpat[0], BLK)
    right_masked = mask_cols(upanel[0], upat[0], BLK)
    right_full = lax.all_gather(right_masked, "row", axis=1, tiled=True)
    update = jnp.einsum(
        "kmw,kwn->mn",
        lax.all_gather(left_masked, "col", axis=2, tiled=True),
        right_full,
        preferred_element_type=jnp.float32,
    )
    share_rows = update.shape[0] // lax.axis_size("layer")
    offset = lax.axis_index("layer") * share_rows
    first = lax.axis_index("layer") == 0
    pivots = jnp.where(first, diagonal(ancestor_entries), 0.0) - diagonal(update)
    diag_lu = factor(lax.psum(pivots, ("layer", "row")))
    total = lax.psum_scatter(update, "layer", scatter_dimension=0, tiled=True)
    schur = lax.dynamic_slice_in_dim(ancestor_entries, offset, share_rows, 0) - total
    return (schur, diag_lu)


def solution(mesh):
    return jax.shard_map(
        shards,
        mesh=mesh,
        in_specs=(
            P("layer", None, "row", "col"),
            P("layer", None, "row", "col"),
            P("layer", None, "row"),
            P("layer", None, "col"),
            P("row", "col"),
        ),
        out_specs=(P(("row", "layer"), "col"), P("col", None, None)),
        check_vma=False,
    )
```

```python
import functools

import jax
import jax.numpy as jnp
from jax import lax
from jax.experimental import pallas as pl
from jax.experimental.pallas import tpu as pltpu
from jax.sharding import PartitionSpec as P

MESH = pl.DeviceIdType.MESH
BLK = 128
SEGMENTS = 4
NX, NY, NZ = 4, 4, 8
SUPER = 8
PIECE = 64
ROWS = 1536
COLS = 768
HALF = COLS // 2
GROUP = 16
PARTS = 3
CHUNKS = NY * PARTS
HEIGHT = NZ * GROUP
STRIP = NZ * GROUP * PARTS


def lu_blocks(ref, count):
    lanes = lax.broadcasted_iota(jnp.int32, (8, BLK), 1)
    subs = lax.broadcasted_iota(jnp.int32, (8, BLK), 0)
    lane = lax.broadcasted_iota(jnp.int32, (1, BLK), 1)
    tiles_all = BLK // 8
    per_segment = tiles_all // SEGMENTS
    for segment in range(SEGMENTS):
        top = segment * per_segment

        def panel(index, carry):
            place = top + index
            first = place * 8
            tops = [ref[b, pl.ds(pl.multiple_of(first, 8), 8), :] for b in range(count)]
            rows = [[] for _ in range(count)]
            scales = [jnp.ones((1, BLK), jnp.float32) for _ in range(count)]
            for j in range(8):
                keep = jnp.logical_and(lane > j, lane + first < BLK)
                for b in range(count):
                    row = tops[b][j : j + 1, :]
                    inverse = 1.0 / row[:, j : j + 1]
                    scaled = jnp.where(keep, row * inverse, 0.0)
                    rows[b].append(scaled)
                    scales[b] = jnp.where(lane == j, inverse, scales[b])
                    column = jnp.where(subs > j, tops[b][:, j : j + 1], 0.0)
                    tops[b] = tops[b] - column * scaled
            for b in range(count):
                lower = jnp.logical_and(subs > lanes, lanes < 8)
                done = jnp.where(lower, tops[b] * scales[b], tops[b])
                ref[b, pl.ds(pl.multiple_of(first, 8), 8), :] = pltpu.roll(done, first, 1)
            for b in range(count):
                for tile in range(top + 1, tiles_all):
                    old = ref[b, tile * 8 : tile * 8 + 8, :]
                    new = old
                    for j in range(8):
                        new = new - new[:, j : j + 1] * rows[b][j]
                    new = pltpu.roll(new * scales[b], BLK - 8, 1)
                    ref[b, tile * 8 : tile * 8 + 8, :] = jnp.where(tile > place, new, old)
            return carry

        lax.fori_loop(0, per_segment, panel, 0)


def kernel(
    l_hbm, r_hbm, lpat, upat, anc_hbm, schur_ref, diag_ref,
    lin, rin, anc, lbuf, rbuf, pbuf, ya, yb, yp, ym, zbuf, zp, zm, sbuf, dbuf,
    hsem, xs, xr, rsend, rrecv, ysend, yrecv, zsend, zrecv, dsend, drecv,
):
    layer, c, x = lax.axis_index("layer"), lax.axis_index("row"), lax.axis_index("col")
    y, z = layer // NZ, layer % NZ
    right, left = (x + 1) % NX, (x + NX - 1) % NX
    up, down = (y + 1) % NY * NZ + z, (y + NY - 1) % NY * NZ + z
    ahead, behind = y * NZ + (z + 1) % NZ, y * NZ + (z + NZ - 1) % NZ

    def strip_of(order):
        return (y + 2 - order - order // 2 + 2 * (order // 3) + NY) % NY

    def remote(src, dst, send, recv, device):
        return pltpu.make_async_remote_copy(
            src_ref=src, dst_ref=dst, send_sem=send, recv_sem=recv, device_id=device, device_id_type=MESH
        )

    def load_left(order):
        strip = strip_of(order)
        return pltpu.make_async_copy(
            l_hbm.at[:, :, pl.ds(pl.multiple_of(strip * STRIP, BLK), STRIP)], lin.at[order], hsem.at[order]
        )

    load_right = pltpu.make_async_copy(r_hbm, rin, hsem.at[4])
    load_anc = pltpu.make_async_copy(anc_hbm.at[pl.ds(pl.multiple_of(layer * 48, 8), 48), :], anc, hsem.at[5])

    def xcopy(kind, t):
        b, s = strip_of(t % NY), t // NY
        if kind == 0:
            src, dst, to = lbuf.at[0, b, s], lbuf.at[1, b, s], right
        elif kind == 1:
            src, dst, to = lbuf.at[0, b, s], lbuf.at[2, b, s], left
        elif kind == 2:
            src, dst, to = lbuf.at[1, b, s, 0:4], lbuf.at[3, b, s, 0:4], right
        else:
            src, dst, to = lbuf.at[2, b, s, 4:8], lbuf.at[3, b, s, 4:8], left
        return remote(src, dst, xs.at[kind, t], xr.at[kind, t], {"col": to})

    def rcopy(h, core):
        return remote(rbuf.at[2 * core + h], rbuf.at[2 * core + h], rsend.at[h], rrecv.at[h], {"row": 1 - c})

    def ycopy(kind, s):
        if kind == 0:
            src, dst, to = pbuf.at[4 * s, :, 0:HALF], ya.at[s], up
        elif kind == 1:
            src, dst, to = pbuf.at[4 * s, :, HALF:COLS], yb.at[s], down
        elif kind == 2:
            src, dst, to = pbuf.at[4 * s + 1], yp.at[s], up
        else:
            src, dst, to = pbuf.at[4 * s + 2], ym.at[s], down
        return remote(src, dst, ysend.at[kind, s], yrecv.at[kind, s], {"layer": to})

    def zcopy(way, s, h):
        if way == 0:
            block, to, landing = (z + 4 - h) % NZ, ahead, zp
            cut = pl.ds(HALF, HALF)
        else:
            block, to, landing = (z + 4 + h) % NZ, behind, zm
            cut = pl.ds(0, HALF)
        if h == 0:
            src, dst = zbuf.at[s, block, :, cut], landing.at[4 * s, :, cut]
        else:
            src, dst = zbuf.at[s, block], landing.at[4 * s + h]
        return remote(src, dst, zsend.at[way, 4 * s + h], zrecv.at[way, 4 * s + h], {"layer": to})

    load_left(0).start()
    load_right.start()
    for order in range(1, NY):
        load_left(order).start()
    load_anc.start()
    barrier = pltpu.get_barrier_semaphore()
    for to in (left, right):
        pl.semaphore_signal(barrier, inc=1, device_id={"col": to}, device_id_type=MESH)
    own = c * (NY * NZ) + layer
    members = 2 * NY * NZ

    def greet(i, carry):
        to = (own + i) % members
        pl.semaphore_signal(
            barrier, inc=1, device_id={"layer": to % (NY * NZ), "row": to // (NY * NZ)}, device_id_type=MESH
        )
        return carry

    lax.fori_loop(1, members, greet, 0)

    def prepare_left(order):
        b = strip_of(order)
        load_left(order).wait()
        for j in range(STRIP // BLK):
            pieces = []
            for k in range(SUPER):
                tile = lin[order, k, :, j * BLK : (j + 1) * BLK]
                pieces.append(jnp.where(lpat[k, 3 * b + j] > 0, tile, jnp.zeros_like(tile)))
            turned = jnp.concatenate(pieces, axis=0).T
            for g in range(8):
                place = 8 * j + g
                lbuf[0, b, place % PARTS, place // PARTS] = turned[g * GROUP : (g + 1) * GROUP, :]

    prepare_left(0)
    pl.semaphore_wait(barrier, members + 1)
    xcopy(0, 0).start()
    xcopy(1, 0).start()
    load_right.wait()
    for k in range(SUPER):
        for j in range(COLS // BLK):
            for h in range(2):
                tile = rin[k, h * PIECE : (h + 1) * PIECE, j * BLK : (j + 1) * BLK]
                rbuf[2 * c + h, k * PIECE : (k + 1) * PIECE, j * BLK : (j + 1) * BLK] = jnp.where(
                    upat[j, k] > 0, tile, jnp.zeros_like(tile)
                )
    for h in range(2):
        rcopy(h, c).start()
    for order in range(1, NY):
        prepare_left(order)
        xcopy(0, order).start()
        xcopy(1, order).start()
    for h in range(2):
        rcopy(h, 1 - c).wait_recv()
    load_anc.wait()

    owner = jnp.logical_and(c == x // 2, y // 2 == x % 2)

    def step(t, carry):
        @pl.when(t < CHUNKS)
        def _():
            xcopy(0, t).wait_recv()
            xcopy(2, t).start()
            xcopy(1, t).wait_recv()
            xcopy(3, t).start()

        @pl.when(t < CHUNKS - NY)
        def _():
            xcopy(0, t + NY).start()
            xcopy(1, t + NY).start()

        @pl.when(jnp.logical_and(t >= 1, t < CHUNKS + 1))
        def _():
            u = t - 1
            xcopy(2, u).wait_recv()
            xcopy(3, u).wait_recv()
            b, s = strip_of(u % NY), u // NY
            for n in range(COLS // 256):
                total = None
                for slot, shift in enumerate((0, 3, 1, 2)):
                    product = jnp.dot(
                        lbuf[slot, b, s].reshape(HEIGHT, SUPER * PIECE),
                        rbuf[(x + shift) % NX, :, n * 256 : (n + 1) * 256],
                        preferred_element_type=jnp.float32,
                    )
                    total = product if total is None else total + product
                pbuf[u, :, n * 256 : (n + 1) * 256] = total

            @pl.when(u % NY == 0)
            def _():
                ycopy(0, s).start()
                ycopy(1, s).start()

        @pl.when(jnp.logical_and(t >= 2, t < CHUNKS + 2))
        def _():
            v = t - 2
            s = v // NY

            @pl.when(v % NY == 1)
            def _():
                ycopy(0, s).wait_recv()
                pbuf[v, :, 0:HALF] = pbuf[v, :, 0:HALF] + ya[s]
                ycopy(2, s).start()

            @pl.when(v % NY == 2)
            def _():
                ycopy(1, s).wait_recv()
                pbuf[v, :, HALF:COLS] = pbuf[v, :, HALF:COLS] + yb[s]
                ycopy(3, s).start()

        @pl.when(jnp.logical_and(t >= 11, t % 4 == 3))
        def _():
            s = (t - 11) // 4
            for way in range(2):
                zcopy(way, s, 3).wait_recv()
            total = zbuf[s, z] + zp[4 * s + 3] + zm[4 * s + 3]
            rows = pl.ds(pl.multiple_of(GROUP * s, GROUP), GROUP)
            final = anc[rows, :] - total
            sbuf[s] = final
            schur_ref[rows, :] = final

            @pl.when(owner)
            def _():
                place = STRIP * (y % 2) + 48 * z + GROUP * s
                j = place // BLK
                cut = pl.ds(pl.multiple_of(j * BLK, BLK), BLK)
                spot = pl.ds(pl.multiple_of(place, GROUP), GROUP)
                dbuf[spot, :] = sbuf[s, :, cut]

                def hand_out(i, carry):
                    to = (own + i) % members
                    remote(
                        sbuf.at[s, :, cut], dbuf.at[spot, :], dsend.at[s], drecv.at[0],
                        {"layer": to % (NY * NZ), "row": to // (NY * NZ)},
                    ).start()
                    return carry

                lax.fori_loop(1, members, hand_out, 0)

        @pl.when(jnp.logical_and(t >= 7, t < 19))
        def _():
            s, h_now = (t - 7) // 4, (t - 7) % 4
            for h in range(4):

                @pl.when(h_now == h)
                def _():
                    if h == 0:
                        ycopy(2, s).wait_recv()
                        ycopy(3, s).wait_recv()
                        zbuf[s] = (pbuf[4 * s + 3] + yp[s] + ym[s]).reshape(NZ, GROUP, COLS)
                    for way in range(2):
                        block = (z + 4 - h) % NZ if way == 0 else (z + 4 + h) % NZ
                        landing = zp if way == 0 else zm
                        cut = slice(HALF, COLS) if way == 0 else slice(0, HALF)
                        if h == 1:
                            zcopy(way, s, 0).wait_recv()
                            zbuf[s, block, :, cut] = zbuf[s, block, :, cut] + landing[4 * s, :, cut]
                        elif h > 1:
                            zcopy(way, s, h - 1).wait_recv()
                            zbuf[s, block] = zbuf[s, block] + landing[4 * s + h - 1]
                        zcopy(way, s, h).start()

        return carry

    lax.fori_loop(0, 20, step, 0)

    @pl.when(owner)
    def _():
        pltpu.make_async_copy(dbuf.at[0:720], dbuf.at[0:720], drecv.at[0]).wait()

    @pl.when(jnp.logical_not(owner))
    def _():
        pltpu.make_async_copy(dbuf, dbuf, drecv.at[0]).wait()

    diag_ref[...] = dbuf[...].reshape(6, BLK, BLK)
    lu_blocks(diag_ref, 6)

    @pl.when(owner)
    def _():
        for s in range(PARTS):
            sent = pbuf.at[0:7, 0:24, :]
            pltpu.make_async_copy(sent, sent, dsend.at[s]).wait()

    for h in range(2):
        rcopy(h, c).wait_send()

    def drain_x(t, carry):
        for kind in range(4):
            xcopy(kind, t).wait_send()
        return carry

    lax.fori_loop(0, CHUNKS, drain_x, 0)

    def drain_yz(s, carry):
        for kind in range(4):
            ycopy(kind, s).wait_send()
        for h in range(4):
            for way in range(2):
                zcopy(way, s, h).wait_send()
        return carry

    lax.fori_loop(0, PARTS, drain_yz, 0)


def shards(lpanel, upanel, lpat, upat, ancestor_entries):
    f32, bf16 = jnp.float32, jnp.bfloat16
    vmem = pl.BlockSpec(memory_space=pltpu.VMEM)
    smem = pl.BlockSpec(memory_space=pltpu.SMEM)
    anywhere = pl.BlockSpec(memory_space=pl.ANY)
    dma = pltpu.SemaphoreType.DMA
    return pl.pallas_call(
        kernel,
        out_shape=(jax.ShapeDtypeStruct((48, COLS), f32), jax.ShapeDtypeStruct((6, BLK, BLK), f32)),
        in_specs=[anywhere, anywhere, smem, smem, anywhere],
        out_specs=(vmem, vmem),
        scratch_shapes=[
            pltpu.VMEM((NY, SUPER, PIECE, STRIP), bf16),
            pltpu.VMEM((SUPER, 2 * PIECE, COLS), bf16),
            pltpu.VMEM((48, COLS), f32),
            pltpu.VMEM((NX, NY, PARTS, NZ, GROUP, SUPER * PIECE), bf16),
            pltpu.VMEM((NX, SUPER * PIECE, COLS), bf16),
            pltpu.VMEM((CHUNKS, HEIGHT, COLS), f32),
            pltpu.VMEM((PARTS, HEIGHT, HALF), f32),
            pltpu.VMEM((PARTS, HEIGHT, HALF), f32),
            pltpu.VMEM((PARTS, HEIGHT, COLS), f32),
            pltpu.VMEM((PARTS, HEIGHT, COLS), f32),
            pltpu.VMEM((PARTS, NZ, GROUP, COLS), f32),
            pltpu.VMEM((4 * PARTS, GROUP, COLS), f32),
            pltpu.VMEM((4 * PARTS, GROUP, COLS), f32),
            pltpu.VMEM((PARTS, GROUP, COLS), f32),
            pltpu.VMEM((6 * BLK, BLK), f32),
            dma((6,)), dma((4, CHUNKS)), dma((4, CHUNKS)), dma((2,)), dma((2,)),
            dma((4, PARTS)), dma((4, PARTS)), dma((2, 4 * PARTS)), dma((2, 4 * PARTS)), dma((PARTS,)), dma((1,)),
        ],
        compiler_params=pltpu.CompilerParams(
            collective_id=0, has_side_effects=True, vmem_limit_bytes=60 * 1024 * 1024
        ),
    )(
        jnp.swapaxes(lpanel[0], 1, 2),
        upanel[0],
        lpat[0],
        jnp.swapaxes(upat[0], 0, 1),
        ancestor_entries,
    )


def solution(mesh):
    return jax.shard_map(
        shards,
        mesh=mesh,
        in_specs=(
            P("layer", None, "row", "col"),
            P("layer", None, "row", "col"),
            P("layer", None, "row"),
            P("layer", None, "col"),
            P("row", "col"),
        ),
        out_specs=(P(("row", "layer"), "col"), P("col", None, None)),
        check_vma=False,
    )
```

```python
import jax
import jax.numpy as jnp
from jax import lax
from jax.experimental import pallas as pl
from jax.experimental.pallas import tpu as pltpu
from jax.sharding import PartitionSpec as P

MESH = pl.DeviceIdType.MESH
BLK = 128
SEGMENTS = 4
NX, NY, NZ = 4, 4, 8
SUPER = 8
PIECE = 64
ROWS = 1536
COLS = 768
HALF = COLS // 2
GROUP = 16
PARTS = 3
CHUNKS = NY * PARTS
HEIGHT = NZ * GROUP
STRIP = NZ * GROUP * PARTS
LEAD = 3
START = 10


def lu_segment(segment, work, out):
    count = out.shape[0]
    lanes = lax.broadcasted_iota(jnp.int32, (8, BLK), 1)
    subs = lax.broadcasted_iota(jnp.int32, (8, BLK), 0)
    total = BLK // 8
    per_segment = total // SEGMENTS
    live = total - segment * per_segment

    def spread(line):
        return jnp.broadcast_to(line, (8, BLK))

    def panel(index, carry):
        first = (segment * per_segment + index) * 8
        tops = [work[b, 0:8, :] for b in range(count)]
        rest = [[work[b, t * 8 : t * 8 + 8, :] for t in range(1, live)] for b in range(count)]
        scales = [jnp.ones((8, BLK), jnp.float32) for _ in range(count)]
        columns = [[spread(tops[b][:, j : j + 1]) for j in range(8)] for b in range(count)]
        for j in range(8):
            keep = jnp.logical_and(lanes > j, lanes + first < BLK)
            for b in range(count):
                inverse = 1.0 / spread(columns[b][j][j : j + 1, :])
                scaled = jnp.where(keep, spread(tops[b][j : j + 1, :]), 0.0) * inverse
                scales[b] = jnp.where(lanes == j, inverse, scales[b])
                below = jnp.where(subs > j, columns[b][j], 0.0)
                tops[b] = tops[b] - below * scaled
                for q in range(j + 1, 8):
                    columns[b][q] = columns[b][q] - below * (spread(columns[b][q][j : j + 1, :]) * inverse)
                for i in range(live - 1):
                    rest[b][i] = rest[b][i] - rest[b][i][:, j : j + 1] * scaled
        lower = jnp.logical_and(subs > lanes, lanes < 8)
        for b in range(count):
            done = jnp.where(lower, tops[b] * scales[b], tops[b])
            out[b, pl.ds(pl.multiple_of(first, 8), 8), :] = pltpu.roll(done, first, 1)
            for i in range(live - 1):
                work[b, i * 8 : i * 8 + 8, :] = pltpu.roll(rest[b][i] * scales[b], BLK - 8, 1)
        return carry

    lax.fori_loop(0, per_segment, panel, 0)


def finish_kernel(schur_ref, part_ref, rest_ref, schur_out, out, work):
    schur_out[...] = schur_ref[...]
    out[...] = part_ref[...]
    work[...] = rest_ref[...]
    lu_segment(SEGMENTS - 1, work, out)


def kernel(
    l_hbm, r_hbm, lpat, upat, anc_hbm, schur_ref, part_ref, rest_ref,
    lin, rin, anc, ancd, lbuf, rbuf, pbuf, ya, yb, yp, ym, zbuf, zp, zm, dpart, dall, dbuf, work,
    hsem, xs, xr, rsend, rrecv, ysend, yrecv, zsend, zrecv, esend, erecv, dsend, drecv, known,
):
    layer, c, x = lax.axis_index("layer"), lax.axis_index("row"), lax.axis_index("col")
    y, z = layer // NZ, layer % NZ
    right, left = (x + 1) % NX, (x + NX - 1) % NX
    up, down = (y + 1) % NY * NZ + z, (y + NY - 1) % NY * NZ + z
    ahead, behind = y * NZ + (z + 1) % NZ, y * NZ + (z + NZ - 1) % NZ

    def strip_of(order):
        return (y + 2 - order - order // 2 + 2 * (order // 3) + NY) % NY

    def place_of(t):
        late = t // 9
        return (1 - late) * (t % 3) + 3 * late, (1 - late) * (t // 3) + late * (t - 9)

    def remote(src, dst, send, recv, device):
        return pltpu.make_async_remote_copy(
            src_ref=src, dst_ref=dst, send_sem=send, recv_sem=recv, device_id=device, device_id_type=MESH
        )

    def load_left(order):
        strip = strip_of(order)
        return pltpu.make_async_copy(
            l_hbm.at[:, :, pl.ds(pl.multiple_of(strip * STRIP, BLK), STRIP)], lin.at[order], hsem.at[order]
        )

    load_right = pltpu.make_async_copy(r_hbm, rin, hsem.at[4])
    load_anc = pltpu.make_async_copy(anc_hbm.at[pl.ds(pl.multiple_of(layer * 48, 8), 48), :], anc, hsem.at[5])

    def xcopy(kind, t):
        order, s = place_of(t)
        b = strip_of(order)
        if kind == 0:
            src, dst, to = lbuf.at[0, b, s], lbuf.at[1, b, s], right
        elif kind == 1:
            src, dst, to = lbuf.at[0, b, s], lbuf.at[2, b, s], left
        elif kind == 2:
            src, dst, to = lbuf.at[1, b, s, 0:4], lbuf.at[3, b, s, 0:4], right
        else:
            src, dst, to = lbuf.at[2, b, s, 4:8], lbuf.at[3, b, s, 4:8], left
        return remote(src, dst, xs.at[kind, t], xr.at[kind, t], {"col": to})

    def rcopy(h, core):
        return remote(rbuf.at[2 * core + h], rbuf.at[2 * core + h], rsend.at[h], rrecv.at[h], {"row": 1 - c})

    def ycopy(kind, s):
        if kind == 0:
            src, dst, to = pbuf.at[3 * s, :, 0:HALF], ya.at[s], up
        elif kind == 1:
            src, dst, to = pbuf.at[3 * s, :, HALF:COLS], yb.at[s], down
        elif kind == 2:
            src, dst, to = pbuf.at[3 * s + 1], yp.at[s], up
        else:
            src, dst, to = pbuf.at[3 * s + 2], ym.at[s], down
        return remote(src, dst, ysend.at[kind, s], yrecv.at[kind, s], {"layer": to})

    def zcopy(way, s, h):
        if way == 0:
            block, to, landing = (z + 4 - h) % NZ, ahead, zp
            cut = pl.ds(HALF, HALF)
        else:
            block, to, landing = (z + 4 + h) % NZ, behind, zm
            cut = pl.ds(0, HALF)
        if h == 0:
            src, dst = zbuf.at[s, block, :, cut], landing.at[4 * s, :, cut]
        else:
            src, dst = zbuf.at[s, block], landing.at[4 * s + h]
        return remote(src, dst, zsend.at[way, 4 * s + h], zrecv.at[way, 4 * s + h], {"layer": to})

    yy = y % 2

    def ecopy(s, i, source, target):
        return remote(dpart.at[s], dall.at[s, source], esend.at[s, i], erecv.at[s, i], {"layer": y * NZ + target})

    def dcopy(s, half, i):
        to = (c * NY + y + i) % (2 * NY)
        return remote(
            dbuf.at[half, :, s], dbuf.at[half, :, s], dsend.at[s, i], drecv.at[half, s],
            {"layer": to % NY * NZ + z, "row": to // NY},
        )

    def load_blocks(j):
        return pltpu.make_async_copy(
            anc_hbm.at[pl.ds(pl.multiple_of(y * STRIP + j * BLK, BLK), BLK), pl.ds(pl.multiple_of((3 * yy + j) * BLK, BLK), BLK)],
            ancd.at[pl.ds(j * BLK, BLK), :],
            hsem.at[6 + j],
        )

    load_left(0).start()
    barrier = pltpu.get_barrier_semaphore()
    for to in ({"col": left}, {"col": right}, {"row": 1 - c}, {"layer": up}, {"layer": down}, {"layer": ahead}, {"layer": behind}):
        pl.semaphore_signal(barrier, inc=1, device_id=to, device_id_type=MESH)
    load_right.start()
    for order in range(1, NY):
        load_left(order).start()
    load_anc.start()
    for j in range(3):
        load_blocks(j).start()

    def tell(i):
        for to in (ahead, behind):
            pl.semaphore_signal(known.at[i], inc=1, device_id={"layer": to}, device_id_type=MESH)

    def prepare_left(order):
        b = strip_of(order)
        load_left(order).wait()
        for j in range(STRIP // BLK):
            pieces = []
            for k in range(SUPER):
                tile = lin[order, k, :, j * BLK : (j + 1) * BLK]
                pieces.append(jnp.where(lpat[k, 3 * b + j] > 0, tile, jnp.zeros_like(tile)))
            turned = jnp.concatenate(pieces, axis=0).T
            for g in range(8):
                place = 8 * j + g
                lbuf[0, b, place % PARTS, place // PARTS] = turned[g * GROUP : (g + 1) * GROUP, :]

    prepare_left(0)
    pl.semaphore_wait(barrier, 7)
    tell(0)
    xcopy(0, 0).start()
    xcopy(1, 0).start()
    load_right.wait()
    for k in range(SUPER):
        for j in range(COLS // BLK):
            for h in range(2):
                tile = rin[k, h * PIECE : (h + 1) * PIECE, j * BLK : (j + 1) * BLK]
                rbuf[2 * c + h, k * PIECE : (k + 1) * PIECE, j * BLK : (j + 1) * BLK] = jnp.where(
                    upat[j, 0, k] > 0, tile, jnp.zeros_like(tile)
                )
    for h in range(2):
        rcopy(h, c).start()
    for order in range(1, NY):
        prepare_left(order)
        if order < LEAD:
            xcopy(0, order).start()
            xcopy(1, order).start()

    owner = jnp.logical_and(c == x // 2, y // 2 == x % 2)

    def sum_y(s):
        ycopy(2, s).wait_recv()
        ycopy(3, s).wait_recv()
        zbuf[s] = (pbuf[9 + s] + yp[s] + ym[s]).reshape(NZ, GROUP, COLS)

        @pl.when(owner)
        def _():
            for block in range(NZ):
                j = 3 * yy + (48 * block + GROUP * s) // BLK
                piece = zbuf[s, block, :, pl.ds(pl.multiple_of(j * BLK, BLK), BLK)]
                dpart[s, block] = piece
                dall[s, z, block] = piece
            for i in range(1, NZ):
                ecopy(s, i, z, (z + i) % NZ).start()

    def share(s):
        @pl.when(owner)
        def _():
            for i in range(1, NZ):
                ecopy(s, i, (z + NZ - i) % NZ, z).wait_recv()
            for block in range(NZ):
                total = dall[s, 0, block]
                for source in range(1, NZ):
                    total = total + dall[s, source, block]
                rows = pl.ds(pl.multiple_of(48 * block + GROUP * s, GROUP), GROUP)
                dbuf[yy, block, s] = ancd[rows, :] - total
            for i in range(1, 2 * NY):
                dcopy(s, yy, i).start()

    def z_step(s, h):
        for way in range(2):
            block = (z + 4 - h) % NZ if way == 0 else (z + 4 + h) % NZ
            landing = zp if way == 0 else zm
            cut = slice(HALF, COLS) if way == 0 else slice(0, HALF)
            if h >= 1:
                zcopy(way, s, h - 1).wait_recv()
            if h == 1:
                zbuf[s, block, :, cut] = zbuf[s, block, :, cut] + landing[4 * s, :, cut]
            elif 1 < h < 4:
                zbuf[s, block] = zbuf[s, block] + landing[4 * s + h - 1]
            if h < 4:
                zcopy(way, s, h).start()
        if h == 4:
            rows = pl.ds(GROUP * s if isinstance(s, int) else pl.multiple_of(GROUP * s, GROUP), GROUP)
            schur_ref[rows, :] = anc[rows, :] - (zbuf[s, z] + zp[4 * s + 3] + zm[4 * s + 3])

    def step(t, carry):
        @pl.when(t < CHUNKS)
        def _():
            xcopy(0, t).wait_recv()
            xcopy(2, t).start()
            xcopy(1, t).wait_recv()
            xcopy(3, t).start()

        @pl.when(t < CHUNKS - LEAD)
        def _():
            xcopy(0, t + LEAD).start()
            xcopy(1, t + LEAD).start()

        for i in range(3):

            @pl.when(t == i + 2)
            def _():
                pl.semaphore_wait(known.at[i], 2)
                if i < 2:
                    tell(i + 1)

        @pl.when(t == 1)
        def _():
            for h in range(2):
                rcopy(h, 1 - c).wait_recv()
            load_anc.wait()
            for j in range(3):
                load_blocks(j).wait()

        @pl.when(jnp.logical_and(t >= 1, t < CHUNKS + 1))
        def _():
            u = t - 1
            xcopy(2, u).wait_recv()
            xcopy(3, u).wait_recv()
            order, s = place_of(u)
            b = strip_of(order)
            for n in range(COLS // 256):
                total = None
                for slot, shift in enumerate((0, 3, 1, 2)):
                    product = jnp.dot(
                        lbuf[slot, b, s].reshape(HEIGHT, SUPER * PIECE),
                        rbuf[(x + shift) % NX, :, n * 256 : (n + 1) * 256],
                        preferred_element_type=jnp.float32,
                    )
                    total = product if total is None else total + product
                pbuf[u, :, n * 256 : (n + 1) * 256] = total

            @pl.when(order == 0)
            def _():
                ycopy(0, s).start()
                ycopy(1, s).start()

            @pl.when(order == 2)
            def _():
                ycopy(1, s).wait_recv()
                pbuf[u, :, HALF:COLS] = pbuf[u, :, HALF:COLS] + yb[s]
                ycopy(3, s).start()

        @pl.when(jnp.logical_and(t >= 2, jnp.logical_and(t < 11, (t - 2) % 3 == 1)))
        def _():
            v = t - 2
            ycopy(0, v // 3).wait_recv()
            pbuf[v, :, 0:HALF] = pbuf[v, :, 0:HALF] + ya[v // 3]
            ycopy(2, v // 3).start()

        for h in range(2, 5):
            late = t - START - h

            @pl.when(jnp.logical_and(late >= 0, late < PARTS))
            def _():
                z_step(late, h)

        for h in range(2):
            early = t - START - h

            @pl.when(jnp.logical_and(early >= 0, early < PARTS))
            def _():
                if h == 0:
                    sum_y(early)
                z_step(early, h)
                if h == 1:
                    share(early)

        return carry

    lax.fori_loop(0, START + PARTS + 1, step, 0)
    z_step(0, 4)
    z_step(1, 3)
    z_step(2, 2)
    for half in range(2):

        @pl.when(jnp.logical_not(jnp.logical_and(owner, yy == half)))
        def _():
            for s in range(PARTS):
                dcopy(s, half, 1).wait_recv()

    work[...] = dbuf[...].reshape(6, BLK, BLK)
    lu_segment(0, work, part_ref)
    z_step(1, 4)
    z_step(2, 3)
    lu_segment(1, work, part_ref)
    z_step(2, 4)
    lu_segment(2, work, part_ref)
    rest_ref[...] = work[:, 0 : BLK // SEGMENTS, :]

    @pl.when(owner)
    def _():
        for s in range(PARTS):
            for i in range(1, NZ):
                ecopy(s, i, z, (z + i) % NZ).wait_send()
            for i in range(1, 2 * NY):
                dcopy(s, yy, i).wait_send()

    for h in range(2):
        rcopy(h, c).wait_send()

    def drain_x(t, carry):
        for kind in range(4):
            xcopy(kind, t).wait_send()
        return carry

    lax.fori_loop(0, CHUNKS, drain_x, 0)

    def drain_yz(s, carry):
        for kind in range(4):
            ycopy(kind, s).wait_send()
        for h in range(4):
            for way in range(2):
                zcopy(way, s, h).wait_send()
        return carry

    lax.fori_loop(0, PARTS, drain_yz, 0)


def shards(lpanel, upanel, lpat, upat, ancestor_entries):
    f32, bf16 = jnp.float32, jnp.bfloat16
    vmem = pl.BlockSpec(memory_space=pltpu.VMEM)
    smem = pl.BlockSpec(memory_space=pltpu.SMEM)
    anywhere = pl.BlockSpec(memory_space=pl.ANY)
    dma = pltpu.SemaphoreType.DMA
    exchange = pl.pallas_call(
        kernel,
        out_shape=(
            jax.ShapeDtypeStruct((48, COLS), f32),
            jax.ShapeDtypeStruct((6, BLK, BLK), f32),
            jax.ShapeDtypeStruct((6, BLK // SEGMENTS, BLK), f32),
        ),
        in_specs=[anywhere, anywhere, smem, smem, anywhere],
        out_specs=(vmem, vmem, vmem),
        scratch_shapes=[
            pltpu.VMEM((NY, SUPER, PIECE, STRIP), bf16),
            pltpu.VMEM((SUPER, 2 * PIECE, COLS), bf16),
            pltpu.VMEM((48, COLS), f32),
            pltpu.VMEM((STRIP, BLK), f32),
            pltpu.VMEM((NX, NY, PARTS, NZ, GROUP, SUPER * PIECE), bf16),
            pltpu.VMEM((NX, SUPER * PIECE, COLS), bf16),
            pltpu.VMEM((CHUNKS, HEIGHT, COLS), f32),
            pltpu.VMEM((PARTS, HEIGHT, HALF), f32),
            pltpu.VMEM((PARTS, HEIGHT, HALF), f32),
            pltpu.VMEM((PARTS, HEIGHT, COLS), f32),
            pltpu.VMEM((PARTS, HEIGHT, COLS), f32),
            pltpu.VMEM((PARTS, NZ, GROUP, COLS), f32),
            pltpu.VMEM((4 * PARTS, GROUP, COLS), f32),
            pltpu.VMEM((4 * PARTS, GROUP, COLS), f32),
            pltpu.VMEM((PARTS, NZ, GROUP, BLK), f32),
            pltpu.VMEM((PARTS, NZ, NZ, GROUP, BLK), f32),
            pltpu.VMEM((2, NZ, PARTS, GROUP, BLK), f32),
            pltpu.VMEM((6, BLK, BLK), f32),
            dma((9,)), dma((4, CHUNKS)), dma((4, CHUNKS)), dma((2,)), dma((2,)),
            dma((4, PARTS)), dma((4, PARTS)), dma((2, 4 * PARTS)), dma((2, 4 * PARTS)),
            dma((PARTS, NZ)), dma((PARTS, NZ)), dma((PARTS, 2 * NY)), dma((2, PARTS)), pltpu.SemaphoreType.REGULAR((3,)),
        ],
        compiler_params=pltpu.CompilerParams(
            collective_id=0, has_side_effects=True, vmem_limit_bytes=60 * 1024 * 1024
        ),
    )
    schur, part, rest = exchange(
        jnp.swapaxes(lpanel[0], 1, 2),
        upanel[0],
        lpat[0],
        jnp.transpose(upat, (2, 0, 1)),
        ancestor_entries,
    )
    return pl.pallas_call(
        finish_kernel,
        out_shape=(jax.ShapeDtypeStruct(schur.shape, f32), jax.ShapeDtypeStruct(part.shape, f32)),
        in_specs=[vmem, vmem, vmem],
        out_specs=(vmem, vmem),
        scratch_shapes=[pltpu.VMEM(rest.shape, f32)],
    )(schur, part, rest)


def solution(mesh):
    return jax.shard_map(
        shards,
        mesh=mesh,
        in_specs=(
            P("layer", None, "row", "col"),
            P("layer", None, "row", "col"),
            P("layer", None, "row"),
            P("layer", None, "col"),
            P("row", "col"),
        ),
        out_specs=(P(("row", "layer"), "col"), P("col", None, None)),
        check_vma=False,
    )
```

```python
import jax
import jax.numpy as jnp
from jax import lax
from jax.experimental import pallas as pl
from jax.experimental.pallas import tpu as pltpu
from jax.sharding import PartitionSpec as P

MESH = pl.DeviceIdType.MESH
BLK = 128
SEGMENTS = 4
NX, NY, NZ = 4, 4, 8
SUPER = 8
PIECE = 64
ROWS = 1536
COLS = 768
HALF = COLS // 2
GROUP = 16
PARTS = 3
CHUNKS = NY * PARTS
HEIGHT = NZ * GROUP
STRIP = NZ * GROUP * PARTS
LEAD = 3
START = 10


def lu_segment(segment, work, out):
    count = out.shape[0]
    lanes = lax.broadcasted_iota(jnp.int32, (8, BLK), 1)
    subs = lax.broadcasted_iota(jnp.int32, (8, BLK), 0)
    total = BLK // 8
    per_segment = total // SEGMENTS
    live = total - segment * per_segment

    def spread(line):
        return jnp.broadcast_to(line, (8, BLK))

    def panel(index, carry):
        first = (segment * per_segment + index) * 8
        tops = [work[b, 0:8, :] for b in range(count)]
        rest = [[work[b, t * 8 : t * 8 + 8, :] for t in range(1, live)] for b in range(count)]
        scales = [jnp.ones((8, BLK), jnp.float32) for _ in range(count)]
        columns = [[spread(tops[b][:, j : j + 1]) for j in range(8)] for b in range(count)]
        for j in range(8):
            keep = jnp.logical_and(lanes > j, lanes + first < BLK)
            for b in range(count):
                inverse = 1.0 / spread(columns[b][j][j : j + 1, :])
                scaled = jnp.where(keep, spread(tops[b][j : j + 1, :]), 0.0) * inverse
                scales[b] = jnp.where(lanes == j, inverse, scales[b])
                below = jnp.where(subs > j, columns[b][j], 0.0)
                tops[b] = tops[b] - below * scaled
                for q in range(j + 1, 8):
                    columns[b][q] = columns[b][q] - below * (spread(columns[b][q][j : j + 1, :]) * inverse)
                for i in range(live - 1):
                    rest[b][i] = rest[b][i] - rest[b][i][:, j : j + 1] * scaled
        lower = jnp.logical_and(subs > lanes, lanes < 8)
        for b in range(count):
            done = jnp.where(lower, tops[b] * scales[b], tops[b])
            out[b, pl.ds(pl.multiple_of(first, 8), 8), :] = pltpu.roll(done, first, 1)
            for i in range(live - 1):
                work[b, i * 8 : i * 8 + 8, :] = pltpu.roll(rest[b][i] * scales[b], BLK - 8, 1)
        return carry

    lax.fori_loop(0, per_segment, panel, 0)


def finish_kernel(schur_ref, part_ref, rest_ref, schur_out, out, work):
    schur_out[...] = schur_ref[...]
    out[...] = part_ref[...]
    work[...] = rest_ref[...]
    lu_segment(SEGMENTS - 1, work, out)


def kernel(
    l_hbm, r_hbm, lpat, upat, anc_hbm, schur_ref, part_ref, rest_ref,
    lin, rin, anc, ancd, lbuf, rbuf, pbuf, ya, yb, yp, ym, zbuf, zp, zm, dpart, dall, dbuf, work,
    hsem, xs, xr, rsend, rrecv, ysend, yrecv, zsend, zrecv, esend, erecv, fsend, frecv, dsend, drecv, known,
):
    layer, c, x = lax.axis_index("layer"), lax.axis_index("row"), lax.axis_index("col")
    y, z = layer // NZ, layer % NZ
    right, left = (x + 1) % NX, (x + NX - 1) % NX
    up, down = (y + 1) % NY * NZ + z, (y + NY - 1) % NY * NZ + z
    ahead, behind = y * NZ + (z + 1) % NZ, y * NZ + (z + NZ - 1) % NZ

    def strip_of(order):
        return (y + 2 - order - order // 2 + 2 * (order // 3) + NY) % NY

    def place_of(t):
        late = t // 9
        return (1 - late) * (t % 3) + 3 * late, (1 - late) * (t // 3) + late * (t - 9)

    def remote(src, dst, send, recv, device):
        return pltpu.make_async_remote_copy(
            src_ref=src, dst_ref=dst, send_sem=send, recv_sem=recv, device_id=device, device_id_type=MESH
        )

    def load_left(order):
        strip = strip_of(order)
        return pltpu.make_async_copy(
            l_hbm.at[:, :, pl.ds(pl.multiple_of(strip * STRIP, BLK), STRIP)], lin.at[order], hsem.at[order]
        )

    load_right = pltpu.make_async_copy(r_hbm, rin, hsem.at[4])
    load_anc = pltpu.make_async_copy(anc_hbm.at[pl.ds(pl.multiple_of(layer * 48, 8), 48), :], anc, hsem.at[5])

    def xcopy(kind, t):
        order, s = place_of(t)
        b = strip_of(order)
        if kind == 0:
            src, dst, to = lbuf.at[0, b, s], lbuf.at[1, b, s], right
        elif kind == 1:
            src, dst, to = lbuf.at[0, b, s], lbuf.at[2, b, s], left
        elif kind == 2:
            src, dst, to = lbuf.at[1, b, s, 0:4], lbuf.at[3, b, s, 0:4], right
        else:
            src, dst, to = lbuf.at[2, b, s, 4:8], lbuf.at[3, b, s, 4:8], left
        return remote(src, dst, xs.at[kind, t], xr.at[kind, t], {"col": to})

    def rcopy(h, core):
        return remote(rbuf.at[2 * core + h], rbuf.at[2 * core + h], rsend.at[h], rrecv.at[h], {"row": 1 - c})

    def ycopy(kind, s):
        if kind == 0:
            src, dst, to = pbuf.at[3 * s, :, 0:HALF], ya.at[s], up
        elif kind == 1:
            src, dst, to = pbuf.at[3 * s, :, HALF:COLS], yb.at[s], down
        elif kind == 2:
            src, dst, to = pbuf.at[3 * s + 1], yp.at[s], up
        else:
            src, dst, to = pbuf.at[3 * s + 2], ym.at[s], down
        return remote(src, dst, ysend.at[kind, s], yrecv.at[kind, s], {"layer": to})

    def zcopy(way, s, h):
        if way == 0:
            block, to, landing = (z + 4 - h) % NZ, ahead, zp
            cut = pl.ds(HALF, HALF)
        else:
            block, to, landing = (z + 4 + h) % NZ, behind, zm
            cut = pl.ds(0, HALF)
        if h == 0:
            src, dst = zbuf.at[s, block, :, cut], landing.at[4 * s, :, cut]
        else:
            src, dst = zbuf.at[s, block], landing.at[4 * s + h]
        return remote(src, dst, zsend.at[way, 4 * s + h], zrecv.at[way, 4 * s + h], {"layer": to})

    yy = y % 2

    def ecopy(s, i, source, target):
        return remote(
            dpart.at[s, target], dall.at[s, source], esend.at[s, i], erecv.at[s, i], {"layer": y * NZ + target}
        )

    def fcopy(s, i, source, target):
        return remote(
            dbuf.at[yy, source, s], dbuf.at[yy, source, s], fsend.at[s, i], frecv.at[s, i], {"layer": y * NZ + target}
        )

    def dcopy(s, half, i):
        to = (c * NY + y + i) % (2 * NY)
        return remote(
            dbuf.at[half, :, s], dbuf.at[half, :, s], dsend.at[s, i], drecv.at[half, s],
            {"layer": to % NY * NZ + z, "row": to // NY},
        )

    def load_blocks(j):
        return pltpu.make_async_copy(
            anc_hbm.at[pl.ds(pl.multiple_of(y * STRIP + j * BLK, BLK), BLK), pl.ds(pl.multiple_of((3 * yy + j) * BLK, BLK), BLK)],
            ancd.at[pl.ds(j * BLK, BLK), :],
            hsem.at[6 + j],
        )

    load_left(0).start()
    barrier = pltpu.get_barrier_semaphore()
    for to in ({"col": left}, {"col": right}, {"row": 1 - c}, {"layer": up}, {"layer": down}, {"layer": ahead}, {"layer": behind}):
        pl.semaphore_signal(barrier, inc=1, device_id=to, device_id_type=MESH)
    load_right.start()
    for order in range(1, NY):
        load_left(order).start()
    load_anc.start()
    for j in range(3):
        load_blocks(j).start()

    def tell(i):
        for to in (ahead, behind):
            pl.semaphore_signal(known.at[i], inc=1, device_id={"layer": to}, device_id_type=MESH)

    def prepare_left(order):
        b = strip_of(order)
        load_left(order).wait()
        for j in range(STRIP // BLK):
            pieces = []
            for k in range(SUPER):
                tile = lin[order, k, :, j * BLK : (j + 1) * BLK]
                pieces.append(jnp.where(lpat[k, 3 * b + j] > 0, tile, jnp.zeros_like(tile)))
            turned = jnp.concatenate(pieces, axis=0).T
            for g in range(8):
                place = 8 * j + g
                lbuf[0, b, place % PARTS, place // PARTS] = turned[g * GROUP : (g + 1) * GROUP, :]

    prepare_left(0)
    pl.semaphore_wait(barrier, 7)
    tell(0)
    xcopy(0, 0).start()
    xcopy(1, 0).start()
    load_right.wait()
    for k in range(SUPER):
        for j in range(COLS // BLK):
            for h in range(2):
                tile = rin[k, h * PIECE : (h + 1) * PIECE, j * BLK : (j + 1) * BLK]
                rbuf[2 * c + h, k * PIECE : (k + 1) * PIECE, j * BLK : (j + 1) * BLK] = jnp.where(
                    upat[j, 0, k] > 0, tile, jnp.zeros_like(tile)
                )
    for h in range(2):
        rcopy(h, c).start()
    for order in range(1, NY):
        prepare_left(order)
        if order < LEAD:
            xcopy(0, order).start()
            xcopy(1, order).start()

    owner = jnp.logical_and(c == x // 2, y // 2 == x % 2)

    def sum_y(s):
        ycopy(2, s).wait_recv()
        ycopy(3, s).wait_recv()
        zbuf[s] = (pbuf[9 + s] + yp[s] + ym[s]).reshape(NZ, GROUP, COLS)

        @pl.when(owner)
        def _():
            for block in range(NZ):
                j = 3 * yy + (48 * block + GROUP * s) // BLK
                dpart[s, block] = zbuf[s, block, :, pl.ds(pl.multiple_of(j * BLK, BLK), BLK)]
            dall[s, z] = dpart[s, z]
            for i in range(1, NZ):
                ecopy(s, i, z, (z + i) % NZ).start()

    def share(s):
        @pl.when(owner)
        def _():
            for i in range(1, NZ):
                ecopy(s, i, (z + NZ - i) % NZ, z).wait_recv()
            total = dall[s, 0]
            for source in range(1, NZ):
                total = total + dall[s, source]
            rows = pl.ds(pl.multiple_of(48 * z + GROUP * s, GROUP), GROUP)
            dbuf[yy, z, s] = ancd[rows, :] - total
            for i in range(1, NZ):
                fcopy(s, i, z, (z + i) % NZ).start()

    def hand_out(s):
        @pl.when(owner)
        def _():
            for i in range(1, NZ):
                fcopy(s, i, (z + NZ - i) % NZ, z).wait_recv()
            for i in range(1, 2 * NY):
                dcopy(s, yy, i).start()

    def z_step(s, h):
        for way in range(2):
            block = (z + 4 - h) % NZ if way == 0 else (z + 4 + h) % NZ
            landing = zp if way == 0 else zm
            cut = slice(HALF, COLS) if way == 0 else slice(0, HALF)
            if h >= 1:
                zcopy(way, s, h - 1).wait_recv()
            if h == 1:
                zbuf[s, block, :, cut] = zbuf[s, block, :, cut] + landing[4 * s, :, cut]
            elif 1 < h < 4:
                zbuf[s, block] = zbuf[s, block] + landing[4 * s + h - 1]
            if h < 4:
                zcopy(way, s, h).start()
        if h == 4:
            rows = pl.ds(GROUP * s if isinstance(s, int) else pl.multiple_of(GROUP * s, GROUP), GROUP)
            schur_ref[rows, :] = anc[rows, :] - (zbuf[s, z] + zp[4 * s + 3] + zm[4 * s + 3])

    def step(t, carry):
        @pl.when(t < CHUNKS)
        def _():
            xcopy(0, t).wait_recv()
            xcopy(2, t).start()
            xcopy(1, t).wait_recv()
            xcopy(3, t).start()

        @pl.when(t < CHUNKS - LEAD)
        def _():
            xcopy(0, t + LEAD).start()
            xcopy(1, t + LEAD).start()

        for i in range(3):

            @pl.when(t == i + 2)
            def _():
                pl.semaphore_wait(known.at[i], 2)
                if i < 2:
                    tell(i + 1)

        @pl.when(t == 1)
        def _():
            for h in range(2):
                rcopy(h, 1 - c).wait_recv()
            load_anc.wait()
            for j in range(3):
                load_blocks(j).wait()

        @pl.when(jnp.logical_and(t >= 1, t < CHUNKS + 1))
        def _():
            u = t - 1
            xcopy(2, u).wait_recv()
            xcopy(3, u).wait_recv()
            order, s = place_of(u)
            b = strip_of(order)
            for n in range(COLS // 256):
                total = None
                for slot, shift in enumerate((0, 3, 1, 2)):
                    product = jnp.dot(
                        lbuf[slot, b, s].reshape(HEIGHT, SUPER * PIECE),
                        rbuf[(x + shift) % NX, :, n * 256 : (n + 1) * 256],
                        preferred_element_type=jnp.float32,
                    )
                    total = product if total is None else total + product
                pbuf[u, :, n * 256 : (n + 1) * 256] = total

            @pl.when(order == 0)
            def _():
                ycopy(0, s).start()
                ycopy(1, s).start()

            @pl.when(order == 2)
            def _():
                ycopy(1, s).wait_recv()
                pbuf[u, :, HALF:COLS] = pbuf[u, :, HALF:COLS] + yb[s]
                ycopy(3, s).start()

        @pl.when(jnp.logical_and(t >= 2, jnp.logical_and(t < 11, (t - 2) % 3 == 1)))
        def _():
            v = t - 2
            ycopy(0, v // 3).wait_recv()
            pbuf[v, :, 0:HALF] = pbuf[v, :, 0:HALF] + ya[v // 3]
            ycopy(2, v // 3).start()

        for h in range(2, 4):
            late = t - START - h

            @pl.when(jnp.logical_and(late >= 0, late < PARTS))
            def _():
                z_step(late, h)

        for h in range(2):
            early = t - START - h

            @pl.when(jnp.logical_and(early >= 0, early < PARTS))
            def _():
                if h == 0:
                    sum_y(early)
                z_step(early, h)
                if h == 1:
                    share(early)

        @pl.when(jnp.logical_and(t >= START + 2, t < START + PARTS))
        def _():
            hand_out(t - START - 2)

        return carry

    lax.fori_loop(0, START + PARTS, step, 0)
    share(2)
    z_step(2, 1)
    hand_out(1)
    hand_out(2)
    z_step(0, 3)
    z_step(1, 2)
    z_step(2, 2)
    z_step(0, 4)
    for half in range(2):

        @pl.when(jnp.logical_not(jnp.logical_and(owner, yy == half)))
        def _():
            for s in range(PARTS):
                dcopy(s, half, 1).wait_recv()

    work[...] = dbuf[...].reshape(6, BLK, BLK)
    lu_segment(0, work, part_ref)
    z_step(1, 3)
    z_step(2, 3)
    lu_segment(1, work, part_ref)
    z_step(1, 4)
    z_step(2, 4)
    lu_segment(2, work, part_ref)
    rest_ref[...] = work[:, 0 : BLK // SEGMENTS, :]

    @pl.when(owner)
    def _():
        for s in range(PARTS):
            for i in range(1, NZ):
                ecopy(s, i, z, (z + i) % NZ).wait_send()
                fcopy(s, i, z, (z + i) % NZ).wait_send()
            for i in range(1, 2 * NY):
                dcopy(s, yy, i).wait_send()

    for h in range(2):
        rcopy(h, c).wait_send()

    def drain_x(t, carry):
        for kind in range(4):
            xcopy(kind, t).wait_send()
        return carry

    lax.fori_loop(0, CHUNKS, drain_x, 0)

    def drain_yz(s, carry):
        for kind in range(4):
            ycopy(kind, s).wait_send()
        for h in range(4):
            for way in range(2):
                zcopy(way, s, h).wait_send()
        return carry

    lax.fori_loop(0, PARTS, drain_yz, 0)


def shards(lpanel, upanel, lpat, upat, ancestor_entries):
    f32, bf16 = jnp.float32, jnp.bfloat16
    vmem = pl.BlockSpec(memory_space=pltpu.VMEM)
    smem = pl.BlockSpec(memory_space=pltpu.SMEM)
    anywhere = pl.BlockSpec(memory_space=pl.ANY)
    dma = pltpu.SemaphoreType.DMA
    exchange = pl.pallas_call(
        kernel,
        out_shape=(
            jax.ShapeDtypeStruct((48, COLS), f32),
            jax.ShapeDtypeStruct((6, BLK, BLK), f32),
            jax.ShapeDtypeStruct((6, BLK // SEGMENTS, BLK), f32),
        ),
        in_specs=[anywhere, anywhere, smem, smem, anywhere],
        out_specs=(vmem, vmem, vmem),
        scratch_shapes=[
            pltpu.VMEM((NY, SUPER, PIECE, STRIP), bf16),
            pltpu.VMEM((SUPER, 2 * PIECE, COLS), bf16),
            pltpu.VMEM((48, COLS), f32),
            pltpu.VMEM((STRIP, BLK), f32),
            pltpu.VMEM((NX, NY, PARTS, NZ, GROUP, SUPER * PIECE), bf16),
            pltpu.VMEM((NX, SUPER * PIECE, COLS), bf16),
            pltpu.VMEM((CHUNKS, HEIGHT, COLS), f32),
            pltpu.VMEM((PARTS, HEIGHT, HALF), f32),
            pltpu.VMEM((PARTS, HEIGHT, HALF), f32),
            pltpu.VMEM((PARTS, HEIGHT, COLS), f32),
            pltpu.VMEM((PARTS, HEIGHT, COLS), f32),
            pltpu.VMEM((PARTS, NZ, GROUP, COLS), f32),
            pltpu.VMEM((4 * PARTS, GROUP, COLS), f32),
            pltpu.VMEM((4 * PARTS, GROUP, COLS), f32),
            pltpu.VMEM((PARTS, NZ, GROUP, BLK), f32),
            pltpu.VMEM((PARTS, NZ, GROUP, BLK), f32),
            pltpu.VMEM((2, NZ, PARTS, GROUP, BLK), f32),
            pltpu.VMEM((6, BLK, BLK), f32),
            dma((9,)), dma((4, CHUNKS)), dma((4, CHUNKS)), dma((2,)), dma((2,)),
            dma((4, PARTS)), dma((4, PARTS)), dma((2, 4 * PARTS)), dma((2, 4 * PARTS)),
            dma((PARTS, NZ)), dma((PARTS, NZ)), dma((PARTS, NZ)), dma((PARTS, NZ)), dma((PARTS, 2 * NY)), dma((2, PARTS)), pltpu.SemaphoreType.REGULAR((3,)),
        ],
        compiler_params=pltpu.CompilerParams(
            collective_id=0, has_side_effects=True, vmem_limit_bytes=60 * 1024 * 1024
        ),
    )
    schur, part, rest = exchange(
        jnp.swapaxes(lpanel[0], 1, 2),
        upanel[0],
        lpat[0],
        jnp.transpose(upat, (2, 0, 1)),
        ancestor_entries,
    )
    return pl.pallas_call(
        finish_kernel,
        out_shape=(jax.ShapeDtypeStruct(schur.shape, f32), jax.ShapeDtypeStruct(part.shape, f32)),
        in_specs=[vmem, vmem, vmem],
        out_specs=(vmem, vmem),
        scratch_shapes=[pltpu.VMEM(rest.shape, f32)],
    )(schur, part, rest)


def solution(mesh):
    return jax.shard_map(
        shards,
        mesh=mesh,
        in_specs=(
            P("layer", None, "row", "col"),
            P("layer", None, "row", "col"),
            P("layer", None, "row"),
            P("layer", None, "col"),
            P("row", "col"),
        ),
        out_specs=(P(("row", "layer"), "col"), P("col", None, None)),
        check_vma=False,
    )
```

```python
import jax
import jax.numpy as jnp
from jax import lax
from jax.experimental import pallas as pl
from jax.experimental.pallas import tpu as pltpu
from jax.sharding import PartitionSpec as P

MESH = pl.DeviceIdType.MESH
BLK = 128
SEGMENTS = 4
NX, NY, NZ = 4, 4, 8
SUPER = 8
PIECE = 64
ROWS = 1536
COLS = 768
HALF = COLS // 2
GROUP = 16
PARTS = 3
CHUNKS = NY * PARTS
HEIGHT = NZ * GROUP
STRIP = NZ * GROUP * PARTS
LEAD = 2
START = 10


def lu_segment(segment, work, out):
    count = out.shape[0]
    lanes = lax.broadcasted_iota(jnp.int32, (8, BLK), 1)
    subs = lax.broadcasted_iota(jnp.int32, (8, BLK), 0)
    total = BLK // 8
    per_segment = total // SEGMENTS
    live = total - segment * per_segment

    def spread(line):
        return jnp.broadcast_to(line, (8, BLK))

    def panel(index, carry):
        first = (segment * per_segment + index) * 8
        tops = [work[b, 0:8, :] for b in range(count)]
        rest = [[work[b, t * 8 : t * 8 + 8, :] for t in range(1, live)] for b in range(count)]
        scales = [jnp.ones((8, BLK), jnp.float32) for _ in range(count)]
        columns = [[spread(tops[b][:, j : j + 1]) for j in range(8)] for b in range(count)]
        for j in range(8):
            keep = jnp.logical_and(lanes > j, lanes + first < BLK)
            for b in range(count):
                inverse = 1.0 / spread(columns[b][j][j : j + 1, :])
                scaled = jnp.where(keep, spread(tops[b][j : j + 1, :]), 0.0) * inverse
                scales[b] = jnp.where(lanes == j, inverse, scales[b])
                below = jnp.where(subs > j, columns[b][j], 0.0)
                tops[b] = tops[b] - below * scaled
                for q in range(j + 1, 8):
                    columns[b][q] = columns[b][q] - below * (spread(columns[b][q][j : j + 1, :]) * inverse)
                for i in range(live - 1):
                    rest[b][i] = rest[b][i] - rest[b][i][:, j : j + 1] * scaled
        lower = jnp.logical_and(subs > lanes, lanes < 8)
        for b in range(count):
            done = jnp.where(lower, tops[b] * scales[b], tops[b])
            out[b, pl.ds(pl.multiple_of(first, 8), 8), :] = pltpu.roll(done, first, 1)
            for i in range(live - 1):
                work[b, i * 8 : i * 8 + 8, :] = pltpu.roll(rest[b][i] * scales[b], BLK - 8, 1)
        return carry

    lax.fori_loop(0, per_segment, panel, 0)


def finish_kernel(schur_ref, part_ref, rest_ref, schur_out, out, work):
    schur_out[...] = schur_ref[...]
    out[...] = part_ref[...]
    work[...] = rest_ref[...]
    lu_segment(SEGMENTS - 1, work, out)


def kernel(
    l_hbm, r_hbm, lpat, upat, anc_hbm, schur_ref, part_ref, rest_ref,
    lin, rin, anc, ancd, lbuf, rbuf, pbuf, ya, yb, yp, ym, zbuf, zp, zm, dpart, dall, dbuf, work,
    hsem, xs, xr, rsend, rrecv, ysend, yrecv, zsend, zrecv, esend, erecv, fsend, frecv, dsend, drecv, known,
):
    layer, c, x = lax.axis_index("layer"), lax.axis_index("row"), lax.axis_index("col")
    y, z = layer // NZ, layer % NZ
    right, left = (x + 1) % NX, (x + NX - 1) % NX
    up, down = (y + 1) % NY * NZ + z, (y + NY - 1) % NY * NZ + z
    ahead, behind = y * NZ + (z + 1) % NZ, y * NZ + (z + NZ - 1) % NZ

    def strip_of(order):
        return (y + 2 - order - order // 2 + 2 * (order // 3) + NY) % NY

    def place_of(t):
        late = t // 9
        return (1 - late) * (t % 3) + 3 * late, (1 - late) * (t // 3) + late * (t - 9)

    def remote(src, dst, send, recv, device):
        return pltpu.make_async_remote_copy(
            src_ref=src, dst_ref=dst, send_sem=send, recv_sem=recv, device_id=device, device_id_type=MESH
        )

    def load_left(order):
        strip = strip_of(order)
        return pltpu.make_async_copy(
            l_hbm.at[:, :, pl.ds(pl.multiple_of(strip * STRIP, BLK), STRIP)], lin.at[order], hsem.at[order]
        )

    load_right = pltpu.make_async_copy(r_hbm, rin, hsem.at[4])
    load_anc = pltpu.make_async_copy(anc_hbm.at[pl.ds(pl.multiple_of(layer * 48, 8), 48), :], anc, hsem.at[5])

    def xcopy(kind, t):
        order, s = place_of(t)
        b = strip_of(order)
        if kind == 0:
            src, dst, to = lbuf.at[0, b, s], lbuf.at[1, b, s], right
        elif kind == 1:
            src, dst, to = lbuf.at[0, b, s], lbuf.at[2, b, s], left
        elif kind == 2:
            src, dst, to = lbuf.at[1, b, s, 0:4], lbuf.at[3, b, s, 0:4], right
        else:
            src, dst, to = lbuf.at[2, b, s, 4:8], lbuf.at[3, b, s, 4:8], left
        return remote(src, dst, xs.at[kind, t], xr.at[kind, t], {"col": to})

    def rcopy(h, core):
        return remote(rbuf.at[2 * core + h], rbuf.at[2 * core + h], rsend.at[h], rrecv.at[h], {"row": 1 - c})

    def ycopy(kind, s):
        if kind == 0:
            src, dst, to = pbuf.at[3 * s, :, 0:HALF], ya.at[s], up
        elif kind == 1:
            src, dst, to = pbuf.at[3 * s, :, HALF:COLS], yb.at[s], down
        elif kind == 2:
            src, dst, to = pbuf.at[3 * s + 1], yp.at[s], up
        else:
            src, dst, to = pbuf.at[3 * s + 2], ym.at[s], down
        return remote(src, dst, ysend.at[kind, s], yrecv.at[kind, s], {"layer": to})

    def zcopy(way, s, h):
        if way == 0:
            block, to, landing = (z + 4 - h) % NZ, ahead, zp
            cut = pl.ds(HALF, HALF)
        else:
            block, to, landing = (z + 4 + h) % NZ, behind, zm
            cut = pl.ds(0, HALF)
        if h == 0:
            src, dst = zbuf.at[s, block, :, cut], landing.at[4 * s, :, cut]
        else:
            src, dst = zbuf.at[s, block], landing.at[4 * s + h]
        return remote(src, dst, zsend.at[way, 4 * s + h], zrecv.at[way, 4 * s + h], {"layer": to})

    yy = y % 2

    def ecopy(s, i, source, target):
        return remote(
            dpart.at[s, target], dall.at[s, source], esend.at[s, i], erecv.at[s, i], {"layer": y * NZ + target}
        )

    def fcopy(s, i, source, target):
        return remote(
            dbuf.at[:, source, s], dbuf.at[:, source, s], fsend.at[s, i], frecv.at[s, i], {"layer": y * NZ + target}
        )

    def dcopy(s, half, i):
        to = (c * NY + y + i) % (2 * NY)
        return remote(
            dbuf.at[half, z, s], dbuf.at[half, z, s], dsend.at[s, i], drecv.at[half, s],
            {"layer": to % NY * NZ + z, "row": to // NY},
        )

    def load_blocks(j):
        return pltpu.make_async_copy(
            anc_hbm.at[pl.ds(pl.multiple_of(y * STRIP + j * BLK, BLK), BLK), pl.ds(pl.multiple_of((3 * yy + j) * BLK, BLK), BLK)],
            ancd.at[pl.ds(j * BLK, BLK), :],
            hsem.at[6 + j],
        )

    load_left(0).start()
    barrier = pltpu.get_barrier_semaphore()
    for to in ({"col": left}, {"col": right}, {"row": 1 - c}, {"layer": up}, {"layer": down}, {"layer": ahead}, {"layer": behind}):
        pl.semaphore_signal(barrier, inc=1, device_id=to, device_id_type=MESH)
    load_right.start()
    for order in range(1, NY):
        load_left(order).start()
    load_anc.start()
    for j in range(3):
        load_blocks(j).start()

    def tell(i):
        for to in (ahead, behind):
            pl.semaphore_signal(known.at[i], inc=1, device_id={"layer": to}, device_id_type=MESH)

    def prepare_left(order):
        b = strip_of(order)
        load_left(order).wait()
        for j in range(STRIP // BLK):
            pieces = []
            for k in range(SUPER):
                tile = lin[order, k, :, j * BLK : (j + 1) * BLK]
                pieces.append(jnp.where(lpat[k, 3 * b + j] > 0, tile, jnp.zeros_like(tile)))
            turned = jnp.concatenate(pieces, axis=0).T
            for g in range(8):
                place = 8 * j + g
                lbuf[0, b, place % PARTS, place // PARTS] = turned[g * GROUP : (g + 1) * GROUP, :]

    prepare_left(0)
    pl.semaphore_wait(barrier, 7)
    tell(0)
    xcopy(0, 0).start()
    xcopy(1, 0).start()
    load_right.wait()
    for k in range(SUPER):
        for j in range(COLS // BLK):
            for h in range(2):
                tile = rin[k, h * PIECE : (h + 1) * PIECE, j * BLK : (j + 1) * BLK]
                rbuf[2 * c + h, k * PIECE : (k + 1) * PIECE, j * BLK : (j + 1) * BLK] = jnp.where(
                    upat[j, 0, k] > 0, tile, jnp.zeros_like(tile)
                )
    for h in range(2):
        rcopy(h, c).start()
    for order in range(1, NY):
        prepare_left(order)
        if order < LEAD:
            xcopy(0, order).start()
            xcopy(1, order).start()

    owner = jnp.logical_and(c == x // 2, y // 2 == x % 2)

    def sum_y(s):
        ycopy(2, s).wait_recv()
        ycopy(3, s).wait_recv()
        zbuf[s] = (pbuf[9 + s] + yp[s] + ym[s]).reshape(NZ, GROUP, COLS)

        @pl.when(owner)
        def _():
            for block in range(NZ):
                j = 3 * yy + (48 * block + GROUP * s) // BLK
                dpart[s, block] = zbuf[s, block, :, pl.ds(pl.multiple_of(j * BLK, BLK), BLK)]
            dall[s, z] = dpart[s, z]
            for i in range(1, NZ):
                ecopy(s, i, z, (z + i) % NZ).start()

    def share(s):
        @pl.when(owner)
        def _():
            for i in range(1, NZ):
                ecopy(s, i, (z + NZ - i) % NZ, z).wait_recv()
            total = dall[s, 0]
            for source in range(1, NZ):
                total = total + dall[s, source]
            rows = pl.ds(pl.multiple_of(48 * z + GROUP * s, GROUP), GROUP)
            dbuf[yy, z, s] = ancd[rows, :] - total
            for i in range(1, 2 * NY):
                dcopy(s, yy, i).start()

    def hand_out(s):
        for half in range(2):

            @pl.when(jnp.logical_not(jnp.logical_and(owner, yy == half)))
            def _():
                dcopy(s, half, 1).wait_recv()

        for i in range(1, NZ):
            fcopy(s, i, z, (z + i) % NZ).start()

    def z_step(s, h):
        for way in range(2):
            block = (z + 4 - h) % NZ if way == 0 else (z + 4 + h) % NZ
            landing = zp if way == 0 else zm
            cut = slice(HALF, COLS) if way == 0 else slice(0, HALF)
            if h >= 1:
                zcopy(way, s, h - 1).wait_recv()
            if h == 1:
                zbuf[s, block, :, cut] = zbuf[s, block, :, cut] + landing[4 * s, :, cut]
            elif 1 < h < 4:
                zbuf[s, block] = zbuf[s, block] + landing[4 * s + h - 1]
            if h < 4:
                zcopy(way, s, h).start()
        if h == 4:
            rows = pl.ds(GROUP * s if isinstance(s, int) else pl.multiple_of(GROUP * s, GROUP), GROUP)
            schur_ref[rows, :] = anc[rows, :] - (zbuf[s, z] + zp[4 * s + 3] + zm[4 * s + 3])

    def step(t, carry):
        @pl.when(t < CHUNKS)
        def _():
            xcopy(0, t).wait_recv()
            xcopy(2, t).start()
            xcopy(1, t).wait_recv()
            xcopy(3, t).start()

        @pl.when(t < CHUNKS - LEAD)
        def _():
            xcopy(0, t + LEAD).start()
            xcopy(1, t + LEAD).start()

        for i in range(3):

            @pl.when(t == i + 2)
            def _():
                pl.semaphore_wait(known.at[i], 2)
                if i < 2:
                    tell(i + 1)

        @pl.when(t == 1)
        def _():
            for h in range(2):
                rcopy(h, 1 - c).wait_recv()
            load_anc.wait()
            for j in range(3):
                load_blocks(j).wait()

        @pl.when(jnp.logical_and(t >= 1, t < CHUNKS + 1))
        def _():
            u = t - 1
            xcopy(2, u).wait_recv()
            xcopy(3, u).wait_recv()
            order, s = place_of(u)
            b = strip_of(order)
            for n in range(COLS // 256):
                total = None
                for slot, shift in enumerate((0, 3, 1, 2)):
                    product = jnp.dot(
                        lbuf[slot, b, s].reshape(HEIGHT, SUPER * PIECE),
                        rbuf[(x + shift) % NX, :, n * 256 : (n + 1) * 256],
                        preferred_element_type=jnp.float32,
                    )
                    total = product if total is None else total + product
                pbuf[u, :, n * 256 : (n + 1) * 256] = total

            @pl.when(order == 0)
            def _():
                ycopy(0, s).start()
                ycopy(1, s).start()

            @pl.when(order == 2)
            def _():
                ycopy(1, s).wait_recv()
                pbuf[u, :, HALF:COLS] = pbuf[u, :, HALF:COLS] + yb[s]
                ycopy(3, s).start()

        @pl.when(jnp.logical_and(t >= 2, jnp.logical_and(t < 11, (t - 2) % 3 == 1)))
        def _():
            v = t - 2
            ycopy(0, v // 3).wait_recv()
            pbuf[v, :, 0:HALF] = pbuf[v, :, 0:HALF] + ya[v // 3]
            ycopy(2, v // 3).start()

        for h in range(2, 4):
            late = t - START - h

            @pl.when(jnp.logical_and(late >= 0, late < PARTS))
            def _():
                z_step(late, h)

        for h in range(2):
            early = t - START - h

            @pl.when(jnp.logical_and(early >= 0, early < PARTS))
            def _():
                if h == 0:
                    sum_y(early)
                z_step(early, h)
                if h == 1:
                    share(early)

        @pl.when(jnp.logical_and(t >= START + 2, t < START + PARTS))
        def _():
            hand_out(t - START - 2)

        return carry

    lax.fori_loop(0, START + PARTS, step, 0)
    share(2)
    z_step(2, 1)
    hand_out(1)
    hand_out(2)
    z_step(0, 3)
    z_step(1, 2)
    z_step(2, 2)
    z_step(0, 4)
    for s in range(PARTS):
        for i in range(1, NZ):
            fcopy(s, i, (z + NZ - i) % NZ, z).wait_recv()

    work[...] = dbuf[...].reshape(6, BLK, BLK)
    lu_segment(0, work, part_ref)
    z_step(1, 3)
    z_step(2, 3)
    lu_segment(1, work, part_ref)
    z_step(1, 4)
    z_step(2, 4)
    lu_segment(2, work, part_ref)
    rest_ref[...] = work[:, 0 : BLK // SEGMENTS, :]

    @pl.when(owner)
    def _():
        for s in range(PARTS):
            for i in range(1, NZ):
                ecopy(s, i, z, (z + i) % NZ).wait_send()
            for i in range(1, 2 * NY):
                dcopy(s, yy, i).wait_send()

    for s in range(PARTS):
        for i in range(1, NZ):
            fcopy(s, i, z, (z + i) % NZ).wait_send()
    for h in range(2):
        rcopy(h, c).wait_send()

    def drain_x(t, carry):
        for kind in range(4):
            xcopy(kind, t).wait_send()
        return carry

    lax.fori_loop(0, CHUNKS, drain_x, 0)

    def drain_yz(s, carry):
        for kind in range(4):
            ycopy(kind, s).wait_send()
        for h in range(4):
            for way in range(2):
                zcopy(way, s, h).wait_send()
        return carry

    lax.fori_loop(0, PARTS, drain_yz, 0)


def shards(lpanel, upanel, lpat, upat, ancestor_entries):
    f32, bf16 = jnp.float32, jnp.bfloat16
    vmem = pl.BlockSpec(memory_space=pltpu.VMEM)
    smem = pl.BlockSpec(memory_space=pltpu.SMEM)
    anywhere = pl.BlockSpec(memory_space=pl.ANY)
    dma = pltpu.SemaphoreType.DMA
    exchange = pl.pallas_call(
        kernel,
        out_shape=(
            jax.ShapeDtypeStruct((48, COLS), f32),
            jax.ShapeDtypeStruct((6, BLK, BLK), f32),
            jax.ShapeDtypeStruct((6, BLK // SEGMENTS, BLK), f32),
        ),
        in_specs=[anywhere, anywhere, smem, smem, anywhere],
        out_specs=(vmem, vmem, vmem),
        scratch_shapes=[
            pltpu.VMEM((NY, SUPER, PIECE, STRIP), bf16),
            pltpu.VMEM((SUPER, 2 * PIECE, COLS), bf16),
            pltpu.VMEM((48, COLS), f32),
            pltpu.VMEM((STRIP, BLK), f32),
            pltpu.VMEM((NX, NY, PARTS, NZ, GROUP, SUPER * PIECE), bf16),
            pltpu.VMEM((NX, SUPER * PIECE, COLS), bf16),
            pltpu.VMEM((CHUNKS, HEIGHT, COLS), f32),
            pltpu.VMEM((PARTS, HEIGHT, HALF), f32),
            pltpu.VMEM((PARTS, HEIGHT, HALF), f32),
            pltpu.VMEM((PARTS, HEIGHT, COLS), f32),
            pltpu.VMEM((PARTS, HEIGHT, COLS), f32),
            pltpu.VMEM((PARTS, NZ, GROUP, COLS), f32),
            pltpu.VMEM((4 * PARTS, GROUP, COLS), f32),
            pltpu.VMEM((4 * PARTS, GROUP, COLS), f32),
            pltpu.VMEM((PARTS, NZ, GROUP, BLK), f32),
            pltpu.VMEM((PARTS, NZ, GROUP, BLK), f32),
            pltpu.VMEM((2, NZ, PARTS, GROUP, BLK), f32),
            pltpu.VMEM((6, BLK, BLK), f32),
            dma((9,)), dma((4, CHUNKS)), dma((4, CHUNKS)), dma((2,)), dma((2,)),
            dma((4, PARTS)), dma((4, PARTS)), dma((2, 4 * PARTS)), dma((2, 4 * PARTS)),
            dma((PARTS, NZ)), dma((PARTS, NZ)), dma((PARTS, NZ)), dma((PARTS, NZ)), dma((PARTS, 2 * NY)), dma((2, PARTS)), pltpu.SemaphoreType.REGULAR((3,)),
        ],
        compiler_params=pltpu.CompilerParams(
            collective_id=0, has_side_effects=True, vmem_limit_bytes=60 * 1024 * 1024
        ),
    )
    schur, part, rest = exchange(
        jnp.swapaxes(lpanel[0], 1, 2),
        upanel[0],
        lpat[0],
        jnp.transpose(upat, (2, 0, 1)),
        ancestor_entries,
    )
    return pl.pallas_call(
        finish_kernel,
        out_shape=(jax.ShapeDtypeStruct(schur.shape, f32), jax.ShapeDtypeStruct(part.shape, f32)),
        in_specs=[vmem, vmem, vmem],
        out_specs=(vmem, vmem),
        scratch_shapes=[pltpu.VMEM(rest.shape, f32)],
    )(schur, part, rest)


def solution(mesh):
    return jax.shard_map(
        shards,
        mesh=mesh,
        in_specs=(
            P("layer", None, "row", "col"),
            P("layer", None, "row", "col"),
            P("layer", None, "row"),
            P("layer", None, "col"),
            P("row", "col"),
        ),
        out_specs=(P(("row", "layer"), "col"), P("col", None, None)),
        check_vma=False,
    )
```
